32 devices in a mesh: gx: 4 (over x, core), yz: 8 (over z, y).
Axes of the slice: x: 2, y: 2, z: 4, core: 2. Of those that a mesh axis runs over, the one named last changes fastest.
Arguments:
- stream: bfloat16 [128, 9216], P('yz', 'gx'), may hold values from -1700 to 1700
- ln_gain: bfloat16 [9216], P('gx'), may hold values from 0.099609375 to 1.8984375
- q_weight: bfloat16 [9216, 12288], P('gx', 'yz'), may hold values from -0.0625 to 0.0625
- kv_weight: bfloat16 [9216, 512], P('gx', 'yz'), may hold values from -0.0625 to 0.0625
- out_weight: bfloat16 [12288, 9216], P('yz', 'gx'), may hold values from -0.0546875 to 0.0546875
- gate_weight: bfloat16 [9216, 36864], P('gx', 'yz'), may hold values from -0.0625 to 0.0625
- up_weight: bfloat16 [9216, 36864], P('gx', 'yz'), may hold values from -0.0625 to 0.0625
- down_weight: bfloat16 [36864, 9216], P('yz', 'gx'), may hold values from -0.03125 to 0.03125
- cache: bfloat16 [128, 1536, 512], P(('gx', 'yz')), may hold values from -620 to 620
- lengths: int32 [128], P(('gx', 'yz')), may hold values from 1 to 1536, as said below
Outputs:
- update: bfloat16 [128, 9216], P('yz', 'gx')
The draws below stay inside these ranges and needn't reach their ends.
Inputs may be any that keep to these rules, and one draw needn't show every extreme that they name: `lengths`: in every draw some sequence has all 1536 slots filled.
All inputs are finite; a program needn't handle non-finite values.
Results may differ from the reference program's by a relative error of at most 0.0082.
Values may be sent and summed in bfloat16 or wider, within the bound.
A program may use at most 192 MiB of HBM per device.

```python
import math
import jax
import jax.numpy as jnp
from jax import lax

D = 9216
HEADS = 48
HEAD_DIM = 256
FF = 36864
CACHE_LEN = 1536
BATCH = 128


def draw_stream(key, part):
    first, second, third = jax.random.split(jax.random.fold_in(key, 11), 3)
    noise = jnp.clip(jax.random.normal(first, (BATCH, D), jnp.float32), -4.0, 4.0)
    row_scale = jnp.exp(jax.random.uniform(second, (BATCH, 1), jnp.float32, 0.0, math.log(10.0)))
    ramp = 1.0 + 2.0 * jnp.arange(D, dtype=jnp.float32)[None, :] / (D - 1)
    col_scale = jnp.exp(jax.random.uniform(third, (1, D), jnp.float32, 0.0, math.log(10.0))) * ramp
    return (noise * row_scale * col_scale).astype(jnp.bfloat16)


def draw_cache(key, part):
    first, second = jax.random.split(jax.random.fold_in(key, 23), 2)
    key_rows = jnp.clip(jax.random.normal(first, (BATCH, CACHE_LEN, HEAD_DIM), jnp.float32), -6.0, 6.0)
    value_rows = jnp.clip(jax.random.normal(second, (BATCH, CACHE_LEN, HEAD_DIM), jnp.float32), -6.0, 6.0)
    return jnp.concatenate([key_rows, value_rows], axis=2).astype(jnp.bfloat16)


def draw_lengths(key, part):
    first, second = jax.random.split(jax.random.fold_in(key, 37))
    drawn = jax.random.randint(first, (BATCH,), 1, CACHE_LEN + 1, jnp.int32)
    where_full = jax.random.randint(second, (), 0, BATCH, jnp.int32)
    return jnp.where(jnp.arange(BATCH, dtype=jnp.int32) == where_full, jnp.int32(CACHE_LEN), drawn)


def block_scale(stream_key, shape, cuts, smallest, high):
    def one(axis_at, parts):
        draws = jax.random.uniform(jax.random.fold_in(jax.random.fold_in(stream_key, 6), axis_at), (parts,), jnp.float32, smallest / len(cuts), high / len(cuts))
        return jnp.repeat(jnp.exp(draws), shape[axis_at] // parts).reshape((-1,) + (1,) * (len(shape) - axis_at - 1))

    factor_of = one(*cuts[0])
    for cut in cuts[1:]:
        factor_of = factor_of * one(*cut)
    return factor_of


def gaussian(stream_key, dims, deviation, limit, cuts=(), kind=jnp.bfloat16):
    loudness = block_scale(stream_key, dims, cuts, -0.22, 0.18) if cuts else 1.0
    values = jax.random.normal(stream_key, dims, jnp.float32) * deviation * loudness
    return jnp.minimum(jnp.maximum(values, -limit), limit).astype(kind)


def setup_inputs(seed: int = 0) -> dict:
    splits = jax.random.split(jax.random.key(seed), 11)
    return {
        "stream": draw_stream(jax.random.fold_in(splits[10], 71), 0),
        "ln_gain": jnp.clip(1.0 + 0.18 * jax.random.normal(splits[1], (D,), jnp.float32), 0.099609375, 1.8984375).astype(jnp.bfloat16),
        "q_weight": gaussian(splits[2], (D, HEADS * HEAD_DIM), D ** -0.5, 0.0625, ((0, 4), (1, 8))),
        "kv_weight": gaussian(splits[3], (D, 2 * HEAD_DIM), D ** -0.5, 0.0625, ((0, 4), (1, 8))),
        "out_weight": gaussian(splits[4], (HEADS * HEAD_DIM, D), (HEADS * HEAD_DIM) ** -0.5, 0.0546875, ((0, 8), (1, 4))),
        "gate_weight": gaussian(splits[5], (D, FF), D ** -0.5, 0.0625, ((0, 4), (1, 8))),
        "up_weight": gaussian(splits[6], (D, FF), D ** -0.5, 0.0625, ((0, 4), (1, 8))),
        "down_weight": gaussian(splits[7], (FF, D), FF ** -0.5, 0.03125, ((0, 8), (1, 4))),
        "cache": draw_cache(jax.random.fold_in(splits[10], 71), 0),
        "lengths": draw_lengths(jax.random.fold_in(splits[10], 71), 0),
    }


def attend_one(query, new_kv, cache, length):
    head_dim = cache.shape[1] // 2
    heads = query.shape[0] // head_dim
    query_vectors = query.reshape(heads, head_dim).astype(jnp.float32)
    key_rows = cache[:, :head_dim].astype(jnp.float32)
    value_rows = cache[:, head_dim:].astype(jnp.float32)
    new_key = new_kv[:head_dim].astype(jnp.float32)
    new_value = new_kv[head_dim:].astype(jnp.float32)
    score_scale = 1.0 / math.sqrt(head_dim)
    attention_logits = jnp.einsum('hd,ld->hl', query_vectors, key_rows) * score_scale
    own = lax.optimization_barrier(jnp.sum(query_vectors * new_key[None, :], axis=1)) * score_scale
    positions = lax.broadcasted_iota(jnp.int32, (1, cache.shape[0]), 1)
    valid = positions < length
    top = jnp.maximum(lax.optimization_barrier(jnp.max(jnp.where(valid, attention_logits, own[:, None]), axis=1)), own)
    weights = jnp.where(valid, jnp.exp(attention_logits - top[:, None]), jnp.float32(0.0))
    own_weight = jnp.exp(own - top)
    denom = lax.optimization_barrier(jnp.sum(weights, axis=1)) + own_weight
    attention_probabilities = (weights / denom[:, None]).astype(jnp.bfloat16)
    own_prob = (own_weight / denom).astype(jnp.bfloat16)
    value_mixture = jnp.einsum('hl,ld->hd', attention_probabilities.astype(jnp.float32), value_rows)
    value_mixture = value_mixture + own_prob.astype(jnp.float32)[:, None] * new_value[None, :]
    return value_mixture.astype(jnp.bfloat16).reshape(heads * head_dim)

def reference(stream, ln_gain, q_weight, kv_weight, out_weight, gate_weight, up_weight, down_weight, cache, lengths):
    values_f = stream.astype(jnp.float32)
    mean = lax.optimization_barrier(jnp.sum(values_f, axis=1)) / D
    variance = lax.optimization_barrier(jnp.sum(values_f * values_f, axis=1)) / D - mean * mean
    normed = ((values_f - mean[:, None]) * lax.rsqrt(variance + 1e-05)[:, None] * ln_gain.astype(jnp.float32)[None, :]).astype(jnp.bfloat16)
    query = jnp.dot(normed, q_weight, preferred_element_type=jnp.float32).astype(jnp.bfloat16)
    new_kv = jnp.dot(normed, kv_weight, preferred_element_type=jnp.float32).astype(jnp.bfloat16)
    attended = lax.map(lambda item: attend_one(item[0], item[1], item[2], item[3]), (query, new_kv, cache, lengths))
    gate = jnp.dot(normed, gate_weight, preferred_element_type=jnp.float32)
    up = jnp.dot(normed, up_weight, preferred_element_type=jnp.float32)
    hidden = (jax.nn.silu(gate) * up).astype(jnp.bfloat16)
    total = jnp.dot(attended, out_weight, preferred_element_type=jnp.float32) + jnp.dot(hidden, down_weight, preferred_element_type=jnp.float32)
    return total.astype(jnp.bfloat16)
```

```python
import functools
import math

import jax
import jax.numpy as jnp
from jax import lax
from jax.experimental import pallas as pl
from jax.experimental.pallas import tpu as pltpu
from jax.sharding import PartitionSpec as P

D = 9216
BF = jnp.bfloat16
F32 = jnp.float32
MESH = pl.DeviceIdType.MESH


def greet(peers):
    barrier = pltpu.get_barrier_semaphore()
    for peer in peers:
        pl.semaphore_signal(barrier, inc=1, device_id=peer, device_id_type=MESH)
    pl.semaphore_wait(barrier, len(peers))


def remote(src, dst, send, recv, peer):
    return pltpu.make_async_remote_copy(
        src_ref=src, dst_ref=dst, send_sem=send, recv_sem=recv,
        device_id=peer, device_id_type=MESH,
    )


class Pairs:
    def __init__(self, axis, n):
        self.axis, self.n, self.half = axis, n, n // 2
        self.me = lax.axis_index(axis)
        self.place = lax.rem(self.me, 2)
        self.row = lax.div(self.me, 2)
        self.partner = {axis: self.me + 1 - 2 * self.place}

    def ahead(self, j):
        return lax.rem(self.row + 1 + j, self.half)

    def behind(self, j):
        return lax.rem(self.row + 2 * self.half - 1 - j, self.half)

    def peer(self, j):
        return {self.axis: 2 * self.ahead(j) + self.place}

    def all(self):
        return [self.partner] + [self.peer(j) for j in range(self.half - 1)]


def gather_start(t, src, out, sa, ra, sb, rb):
    copies = []
    for j in range(t.half - 1):
        c = remote(src, out.at[t.me], sa.at[j], ra.at[j], t.peer(j))
        c.start()
        copies.append(c)
    c = remote(src, out.at[t.me], sb.at[0], rb.at[0], t.partner)
    c.start()
    return copies, [c]


def gather_finish(t, out, sa, ra, sb, rb, started):
    first, second = started
    for j in range(t.half - 1):
        got = 2 * t.behind(j) + t.place
        remote(out.at[got], out.at[got], sa.at[j], ra.at[j], t.peer(j)).wait_recv()
        c = remote(out.at[got], out.at[got], sb.at[1 + j], rb.at[1 + j], t.partner)
        c.start()
        second.append(c)
    for c in first:
        c.wait_send()
    for c in second:
        c.wait()


def norm_kernel(ngx, nyz, x_ref, gain_ref, out_ref, stat, got, ss, sr, sa, ra, sb, rb):
    gx = lax.axis_index("gx")
    t = Pairs("yz", nyz)
    others = [{"gx": lax.rem(gx + 1 + j, ngx)} for j in range(ngx - 1)]
    rows = x_ref.shape[0]
    x = x_ref[...].astype(F32)
    stat[0] = jnp.broadcast_to(jnp.sum(x, axis=1, keepdims=True), (rows, 128))
    stat[1] = jnp.broadcast_to(jnp.sum(x * x, axis=1, keepdims=True), (rows, 128))
    greet(others + t.all())
    copies = []
    for j in range(ngx - 1):
        c = remote(stat, got.at[j], ss.at[j], sr.at[j], others[j])
        c.start()
        copies.append(c)
    for c in copies:
        c.wait()
    total = stat[0]
    squares = stat[1]
    for j in range(ngx - 1):
        total = total + got[j, 0]
        squares = squares + got[j, 1]
    mean = total[:, :1] / D
    var = squares[:, :1] / D - mean * mean
    normed = (x - mean) * lax.rsqrt(var + 1e-05) * gain_ref[...].astype(F32)
    out_ref[t.me] = normed.astype(BF)
    started = gather_start(t, out_ref.at[t.me], out_ref, sa, ra, sb, rb)
    gather_finish(t, out_ref, sa, ra, sb, rb, started)


DMA = pltpu.SemaphoreType.DMA
VM = pl.BlockSpec(memory_space=pltpu.VMEM)


def params(cid):
    return pltpu.CompilerParams(
        collective_id=cid, has_side_effects=True, vmem_limit_bytes=48 * 1024 * 1024
    )


def norm_gather(x, gain, ngx, nyz):
    rows, cols = x.shape
    h = nyz // 2
    out = pl.pallas_call(
        functools.partial(norm_kernel, ngx, nyz),
        out_shape=jax.ShapeDtypeStruct((nyz, rows, cols), BF),
        in_specs=[VM, VM],
        out_specs=VM,
        scratch_shapes=[
            pltpu.VMEM((2, rows, 128), F32),
            pltpu.VMEM((ngx - 1, 2, rows, 128), F32),
            DMA((ngx - 1,)), DMA((ngx - 1,)),
            DMA((max(h - 1, 1),)), DMA((max(h - 1, 1),)), DMA((h,)), DMA((h,)),
        ],
        compiler_params=params(0),
        name="norm_gather",
    )(x, gain.reshape(1, cols))
    return out.reshape(nyz * rows, cols)


def reduce_start(t, x_ref, recv1, s1, r1):
    copies = []
    for j in range(t.half):
        k = t.ahead(j)
        c = remote(x_ref.at[2 * k + 1 - t.place], recv1.at[j], s1.at[j], r1.at[j], t.partner)
        c.start()
        copies.append(c)
    return copies


def reduce_rest(t, x_ref, recv1, stage, recv2, s2, r2, first):
    second = []
    for j in range(t.half - 1):
        k = t.ahead(j)
        first[j].wait_recv()
        stage[j] = (x_ref[2 * k + t.place].astype(F32) + recv1[j].astype(F32)).astype(BF)
        c = remote(stage.at[j], recv2.at[j], s2.at[j], r2.at[j], t.peer(j))
        c.start()
        second.append(c)
    first[t.half - 1].wait_recv()
    total = x_ref[t.me].astype(F32) + recv1[t.half - 1].astype(F32)
    for j in range(t.half - 1):
        second[j].wait_recv()
        total = total + recv2[j].astype(F32)
    for c in first + second:
        c.wait_send()
    return total


def reduce_kernel(axis, n, x_ref, out_ref, recv1, stage, recv2, s1, r1, s2, r2):
    t = Pairs(axis, n)
    greet(t.all())
    first = reduce_start(t, x_ref, recv1, s1, r1)
    out_ref[...] = reduce_rest(t, x_ref, recv1, stage, recv2, s2, r2, first).astype(out_ref.dtype)


def reduce_scratch(n, r, c):
    h = n // 2
    g = max(h - 1, 1)
    return [
        pltpu.VMEM((h, r, c), BF), pltpu.VMEM((g, r, c), BF), pltpu.VMEM((g, r, c), BF),
        DMA((h,)), DMA((h,)), DMA((g,)), DMA((g,)),
    ]


def reduce_scatter(x, axis, n, cid, dtype):
    rows, cols = x.shape
    r = rows // n
    return pl.pallas_call(
        functools.partial(reduce_kernel, axis, n),
        out_shape=jax.ShapeDtypeStruct((r, cols), dtype),
        in_specs=[VM],
        out_specs=VM,
        scratch_shapes=reduce_scratch(n, r, cols),
        compiler_params=params(cid),
        name="reduce_" + axis + str(cid),
    )(x.reshape(n, r, cols))


def gated_kernel(n, x_ref, out_ref, recv1, stage, recv2, s1, r1, s2, r2, sa, ra, sb, rb):
    t = Pairs("gx", n)
    greet(t.all())
    first = reduce_start(t, x_ref, recv1, s1, r1)
    both = reduce_rest(t, x_ref, recv1, stage, recv2, s2, r2, first)
    w = both.shape[1] // 2
    out_ref[t.me] = (jax.nn.silu(both[:, :w]) * both[:, w:]).astype(BF)
    started = gather_start(t, out_ref.at[t.me], out_ref, sa, ra, sb, rb)
    gather_finish(t, out_ref, sa, ra, sb, rb, started)


def gated(x, n, cid):
    rows, cols = x.shape
    r, h = rows // n, n // 2
    g = max(h - 1, 1)
    out = pl.pallas_call(
        functools.partial(gated_kernel, n),
        out_shape=jax.ShapeDtypeStruct((n, r, cols // 2), BF),
        in_specs=[VM],
        out_specs=VM,
        scratch_shapes=reduce_scratch(n, r, cols) + [DMA((g,)), DMA((g,)), DMA((h,)), DMA((h,))],
        compiler_params=params(cid),
        name="gated",
    )(x.reshape(n, r, cols))
    return out.reshape(rows, cols // 2)


def swap_kernel(axis, n, x_ref, out_ref, ss, rs):
    me = lax.axis_index(axis)
    peers = [{axis: lax.rem(me + 1 + j, n)} for j in range(n - 1)]
    greet(peers)
    copies = []
    for j in range(n - 1):
        c = remote(x_ref.at[lax.rem(me + 1 + j, n)], out_ref.at[me], ss.at[j], rs.at[j], peers[j])
        c.start()
        copies.append(c)
    out_ref[me] = x_ref[me]
    for c in copies:
        c.wait()


def swap(x, axis, n, cid):
    return pl.pallas_call(
        functools.partial(swap_kernel, axis, n),
        out_shape=jax.ShapeDtypeStruct(x.shape, x.dtype),
        in_specs=[VM],
        out_specs=VM,
        scratch_shapes=[DMA((n - 1,)), DMA((n - 1,))],
        compiler_params=params(cid),
        name="swap_" + str(cid),
    )(x)


def gather_kernel(axis, n, x_ref, out_ref, sa, ra, sb, rb):
    t = Pairs(axis, n)
    greet(t.all())
    started = gather_start(t, x_ref, out_ref, sa, ra, sb, rb)
    out_ref[t.me] = x_ref[...]
    gather_finish(t, out_ref, sa, ra, sb, rb, started)


def gather(x, axis, n, cid):
    h = n // 2
    g = max(h - 1, 1)
    return pl.pallas_call(
        functools.partial(gather_kernel, axis, n),
        out_shape=jax.ShapeDtypeStruct((n,) + x.shape, x.dtype),
        in_specs=[VM],
        out_specs=VM,
        scratch_shapes=[DMA((g,)), DMA((g,)), DMA((h,)), DMA((h,))],
        compiler_params=params(cid),
        name="gather_" + str(cid),
    )(x)


def attend_local(query, new_kv, cache, lengths):
    seqs = query.shape[0]
    head_dim = cache.shape[2] // 2
    heads = query.shape[1] // head_dim
    query_vectors = query.reshape(seqs, heads, head_dim)
    key_rows = cache[:, :, :head_dim]
    value_rows = cache[:, :, head_dim:]
    new_key = new_kv[:, :head_dim]
    new_value = new_kv[:, head_dim:]
    score_scale = 1.0 / math.sqrt(head_dim)
    attention_logits = (
        jnp.einsum("tgb,twb->tgw", query_vectors, key_rows, preferred_element_type=jnp.float32)
        * score_scale
    )
    own = (
        jnp.einsum("shd,sd->sh", query_vectors, new_key, preferred_element_type=jnp.float32)
        * score_scale
    )
    positions = lax.broadcasted_iota(jnp.int32, (1, 1, cache.shape[1]), 2)
    valid = positions < lengths[:, None, None]
    top = jnp.maximum(jnp.max(jnp.where(valid, attention_logits, own[:, :, None]), axis=2), own)
    weights = jnp.where(valid, jnp.exp(attention_logits - top[:, :, None]), jnp.float32(0.0))
    own_weight = jnp.exp(own - top)
    denom = jnp.sum(weights, axis=2) + own_weight
    attention_probabilities = (weights / denom[:, :, None]).astype(jnp.bfloat16)
    own_prob = (own_weight / denom).astype(jnp.bfloat16)
    value_mixture = jnp.einsum(
        "aqc,acn->aqn", attention_probabilities, value_rows, preferred_element_type=jnp.float32
    )
    value_mixture = (
        value_mixture
        + own_prob.astype(jnp.float32)[:, :, None] * new_value.astype(jnp.float32)[:, None, :]
    )
    return value_mixture.astype(jnp.bfloat16).reshape(seqs, heads * head_dim)


def body(ngx, nyz, stream, ln_gain, q_weight, kv_weight, out_weight, gate_weight, up_weight,
         down_weight, cache, lengths):
    normed = norm_gather(stream, ln_gain, ngx, nyz)
    batch = normed.shape[0]
    qc, kc = q_weight.shape[1], kv_weight.shape[1]
    pad = -(qc + kc) % 128
    seqs = batch // ngx // nyz

    q_part = jnp.dot(normed, q_weight, preferred_element_type=F32).astype(BF)
    kv_part = jnp.dot(normed, kv_weight, preferred_element_type=F32).astype(BF)
    qkv = jnp.concatenate([q_part, kv_part, jnp.zeros((batch, pad), BF)], axis=1)
    qkv_block = reduce_scatter(qkv, "gx", ngx, 1, BF)
    qkv_own = swap(qkv_block.reshape(nyz, seqs, qc + kc + pad), "yz", nyz, 2)
    qkv_own = jnp.swapaxes(qkv_own, 0, 1)
    query_own = qkv_own[:, :, :qc].reshape(seqs, nyz * qc)
    kv_own = qkv_own[:, :, qc:qc + kc].reshape(seqs, nyz * kc)
    attended = attend_local(query_own, kv_own, cache, lengths)
    blocks = jnp.swapaxes(attended.reshape(seqs, nyz, qc), 0, 1)
    head_block = swap(blocks, "yz", nyz, 3).reshape(nyz * seqs, qc)
    head_all = gather(head_block, "gx", ngx, 4).reshape(batch, qc)

    gate_part = jnp.dot(normed, gate_weight, preferred_element_type=F32).astype(BF)
    up_part = jnp.dot(normed, up_weight, preferred_element_type=F32).astype(BF)
    hidden = gated(jnp.concatenate([gate_part, up_part], axis=1), ngx, 5)
    part = jnp.dot(head_all, out_weight, preferred_element_type=F32) + jnp.dot(
        hidden, down_weight, preferred_element_type=F32
    )
    update = reduce_scatter(part.astype(BF), "yz", nyz, 6, F32)
    return update.astype(BF)


def solution(mesh):
    ngx, nyz = mesh.shape["gx"], mesh.shape["yz"]
    return jax.shard_map(
        functools.partial(body, ngx, nyz),
        mesh=mesh,
        in_specs=(
            P("yz", "gx"),
            P("gx"),
            P("gx", "yz"),
            P("gx", "yz"),
            P("yz", "gx"),
            P("gx", "yz"),
            P("gx", "yz"),
            P("yz", "gx"),
            P(("gx", "yz"), None, None),
            P(("gx", "yz")),
        ),
        out_specs=P("yz", "gx"),
        check_vma=False,
    )
```

```python
import functools
import math

import jax
import jax.numpy as jnp
from jax import lax
from jax.experimental import pallas as pl
from jax.experimental.pallas import tpu as pltpu
from jax.sharding import PartitionSpec as P

D = 9216
BF = jnp.bfloat16
F32 = jnp.float32
MESH = pl.DeviceIdType.MESH


def greet(peers):
    barrier = pltpu.get_barrier_semaphore()
    for peer in peers:
        pl.semaphore_signal(barrier, inc=1, device_id=peer, device_id_type=MESH)
    pl.semaphore_wait(barrier, len(peers))


def remote(src, dst, send, recv, peer):
    return pltpu.make_async_remote_copy(
        src_ref=src, dst_ref=dst, send_sem=send, recv_sem=recv,
        device_id=peer, device_id_type=MESH,
    )


class Pairs:
    def __init__(self, axis, n):
        self.axis, self.n, self.half = axis, n, n // 2
        self.me = lax.axis_index(axis)
        self.place = lax.rem(self.me, 2)
        self.row = lax.div(self.me, 2)
        self.partner = {axis: self.me + 1 - 2 * self.place}

    def ahead(self, j):
        return lax.rem(self.row + 1 + j, self.half)

    def behind(self, j):
        return lax.rem(self.row + 2 * self.half - 1 - j, self.half)

    def peer(self, j):
        return {self.axis: 2 * self.ahead(j) + self.place}

    def all(self):
        return [self.partner] + [self.peer(j) for j in range(self.half - 1)]


def gather_start(t, src, out, sa, ra, sb, rb):
    copies = []
    for j in range(t.half - 1):
        c = remote(src, out.at[t.me], sa.at[j], ra.at[j], t.peer(j))
        c.start()
        copies.append(c)
    c = remote(src, out.at[t.me], sb.at[0], rb.at[0], t.partner)
    c.start()
    return copies, [c]


def gather_finish(t, out, sa, ra, sb, rb, started):
    first, second = started
    for j in range(t.half - 1):
        got = 2 * t.behind(j) + t.place
        remote(out.at[got], out.at[got], sa.at[j], ra.at[j], t.peer(j)).wait_recv()
        c = remote(out.at[got], out.at[got], sb.at[1 + j], rb.at[1 + j], t.partner)
        c.start()
        second.append(c)
    for c in first:
        c.wait_send()
    for c in second:
        c.wait()


def norm_kernel(ngx, nyz, x_ref, gain_ref, out_ref, stat, got, ss, sr, sa, ra, sb, rb):
    gx = lax.axis_index("gx")
    t = Pairs("yz", nyz)
    others = [{"gx": lax.rem(gx + 1 + j, ngx)} for j in range(ngx - 1)]
    rows = x_ref.shape[0]
    x = x_ref[...].astype(F32)
    stat[0] = jnp.broadcast_to(jnp.sum(x, axis=1, keepdims=True), (rows, 128))
    stat[1] = jnp.broadcast_to(jnp.sum(x * x, axis=1, keepdims=True), (rows, 128))
    greet(others + t.all())
    copies = []
    for j in range(ngx - 1):
        c = remote(stat, got.at[j], ss.at[j], sr.at[j], others[j])
        c.start()
        copies.append(c)
    for c in copies:
        c.wait()
    total = stat[0]
    squares = stat[1]
    for j in range(ngx - 1):
        total = total + got[j, 0]
        squares = squares + got[j, 1]
    mean = total[:, :1] / D
    var = squares[:, :1] / D - mean * mean
    normed = (x - mean) * lax.rsqrt(var + 1e-05) * gain_ref[...].astype(F32)
    out_ref[t.me] = normed.astype(BF)
    started = gather_start(t, out_ref.at[t.me], out_ref, sa, ra, sb, rb)
    gather_finish(t, out_ref, sa, ra, sb, rb, started)


DMA = pltpu.SemaphoreType.DMA
VM = pl.BlockSpec(memory_space=pltpu.VMEM)


def params(cid):
    return pltpu.CompilerParams(
        collective_id=cid, has_side_effects=True, vmem_limit_bytes=48 * 1024 * 1024
    )


def norm_gather(x, gain, ngx, nyz):
    rows, cols = x.shape
    h = nyz // 2
    out = pl.pallas_call(
        functools.partial(norm_kernel, ngx, nyz),
        out_shape=jax.ShapeDtypeStruct((nyz, rows, cols), BF),
        in_specs=[VM, VM],
        out_specs=VM,
        scratch_shapes=[
            pltpu.VMEM((2, rows, 128), F32),
            pltpu.VMEM((ngx - 1, 2, rows, 128), F32),
            DMA((ngx - 1,)), DMA((ngx - 1,)),
            DMA((max(h - 1, 1),)), DMA((max(h - 1, 1),)), DMA((h,)), DMA((h,)),
        ],
        compiler_params=params(0),
        name="norm_gather",
    )(x, gain.reshape(1, cols))
    return out.reshape(nyz * rows, cols)


def reduce_start(t, x_ref, recv1, s1, r1):
    copies = []
    for j in range(t.half):
        k = t.ahead(j)
        c = remote(x_ref.at[2 * k + 1 - t.place], recv1.at[j], s1.at[j], r1.at[j], t.partner)
        c.start()
        copies.append(c)
    return copies


class Reduce:
    def __init__(self, t, x, recv1, stage, recv2, s1, r1, s2, r2):
        self.t, self.x, self.recv1, self.stage, self.recv2 = t, x, recv1, stage, recv2
        self.s1, self.r1, self.s2, self.r2 = s1, r1, s2, r2

    def start(self):
        self.first = reduce_start(self.t, self.x, self.recv1, self.s1, self.r1)

    def pass_on(self):
        t = self.t
        self.second = []
        for j in range(t.half - 1):
            k = t.ahead(j)
            self.first[j].wait_recv()
            self.stage[j] = (
                self.x[2 * k + t.place].astype(F32) + self.recv1[j].astype(F32)
            ).astype(BF)
            c = remote(self.stage.at[j], self.recv2.at[j], self.s2.at[j], self.r2.at[j], t.peer(j))
            c.start()
            self.second.append(c)

    def total(self):
        t = self.t
        self.first[t.half - 1].wait_recv()
        total = self.x[t.me].astype(F32) + self.recv1[t.half - 1].astype(F32)
        for j in range(t.half - 1):
            self.second[j].wait_recv()
            total = total + self.recv2[j].astype(F32)
        return total

    def end(self):
        for c in self.first + self.second:
            c.wait_send()


class Gather:
    def __init__(self, t, view, sa, ra, sb, rb):
        self.t, self.view = t, view
        self.sa, self.ra, self.sb, self.rb = sa, ra, sb, rb

    def start(self):
        t, own = self.t, self.view(self.t.me)
        self.first = []
        for j in range(t.half - 1):
            c = remote(own, own, self.sa.at[j], self.ra.at[j], t.peer(j))
            c.start()
            self.first.append(c)
        c = remote(own, own, self.sb.at[0], self.rb.at[0], t.partner)
        c.start()
        self.second = [c]

    def pass_on(self):
        t = self.t
        for j in range(t.half - 1):
            got = self.view(2 * t.behind(j) + t.place)
            remote(got, got, self.sa.at[j], self.ra.at[j], t.peer(j)).wait_recv()
            c = remote(got, got, self.sb.at[1 + j], self.rb.at[1 + j], t.partner)
            c.start()
            self.second.append(c)

    def end(self):
        for c in self.first:
            c.wait_send()
        for c in self.second:
            c.wait()


class Swap:
    def __init__(self, axis, n, src, dst, ss, rs):
        self.me = lax.axis_index(axis)
        self.n, self.src, self.dst, self.ss, self.rs = n, src, dst, ss, rs
        self.ids = [lax.rem(self.me + 1 + j, n) for j in range(n - 1)]
        self.peers = [{axis: i} for i in self.ids]

    def start(self):
        self.copies = []
        for j in range(self.n - 1):
            c = remote(
                self.src.at[self.ids[j]], self.dst.at[self.me], self.ss.at[j], self.rs.at[j],
                self.peers[j],
            )
            c.start()
            self.copies.append(c)
        self.dst[self.me] = self.src[self.me]

    def end(self):
        for c in self.copies:
            c.wait()


def first_kernel(ngx, nyz, w, x_ref, kv_ref, qw, gw, uw, hid, own,
                 wbuf, wsem, qx, q1, qs, q2, qsem1, qsem2, qsem3, qsem4, sw, ssem, rsem,
                 px, p1, ps, p2, psem1, psem2, psem3, psem4, sa, ra, sb, rb):
    t = Pairs("gx", ngx)
    qc, ff = qw.shape[1], gw.shape[1]
    nq, nc = qc // w, ff // w
    r = hid.shape[1]
    slots = wbuf.shape[0]
    tiles = [(qw, i) for i in range(nq)]
    for c in range(nc):
        tiles += [(gw, c), (uw, c)]

    def fetch(i):
        ref, c = tiles[i]
        return pltpu.make_async_copy(ref.at[:, pl.ds(c * w, w)], wbuf.at[i % slots], wsem.at[i % slots])

    for i in range(min(slots, len(tiles))):
        fetch(i).start()
    swap = Swap("yz", nyz, sw, own, ssem, rsem)
    greet(t.all() + swap.peers)

    jobs = {}

    def at(step, f):
        jobs.setdefault(step, []).append(f)

    qred = Reduce(t, qx, q1, qs, q2, qsem1, qsem2, qsem3, qsem4)
    reds = [
        Reduce(t, px.at[c], p1.at[c], ps.at[c], p2.at[c], psem1.at[c], psem2.at[c], psem3.at[c], psem4.at[c])
        for c in range(nc)
    ]
    gats = [
        Gather(t, lambda i, c=c: hid.at[i, :, pl.ds(c * w, w)], sa.at[c], ra.at[c], sb.at[c], rb.at[c])
        for c in range(nc)
    ]

    def q_total():
        total = qred.total()
        seqs = sw.shape[1]
        for i in range(nyz):
            sw[i] = total[i * seqs:(i + 1) * seqs].astype(BF)
        swap.start()

    def h_total(c):
        both = reds[c].total()
        hid[t.me, :, c * w:(c + 1) * w] = (jax.nn.silu(both[:, :w]) * both[:, w:]).astype(BF)
        gats[c].start()

    at(nq - 1, qred.start)
    at(nq, qred.pass_on)
    at(nq + 2, q_total)
    for c in range(nc):
        s = nq + 2 * c + 1
        at(s, reds[c].start)
        at(s + 1, reds[c].pass_on)
        at(s + 3, lambda c=c: h_total(c))
        at(s + 5, gats[c].pass_on)

    x = x_ref[...]
    for i in range(max(jobs) + 1):
        if i < len(tiles):
            fetch(i).wait()
            y = jnp.dot(x, wbuf[i % slots], preferred_element_type=F32).astype(BF).reshape(ngx, r, w)
            if i < nq:
                qx[:, :, i * w:(i + 1) * w] = y
            else:
                side = (i - nq) % 2
                px[(i - nq) // 2, :, :, side * w:(side + 1) * w] = y
            if i + slots < len(tiles):
                fetch(i + slots).start()
            if i == nq - 1:
                qx[:, :, qc:] = kv_ref[...].reshape(ngx, r, kv_ref.shape[1])
        for f in jobs.get(i, []):
            f()
    for c in range(nc):
        reds[c].end()
        gats[c].end()
    qred.end()
    swap.end()


def first(x, kv, qw, gw, uw, ngx, nyz):
    batch, depth = x.shape
    qc, ff = qw.shape[1], gw.shape[1]
    w = 768 if qc % 768 == 0 and ff % 768 == 0 else 384
    nc = ff // w
    r, h = batch // ngx, ngx // 2
    g = max(h - 1, 1)
    seqs = r // nyz
    width = qc + kv.shape[1]
    slots = 4
    ANY = pl.BlockSpec(memory_space=pl.ANY)
    return pl.pallas_call(
        functools.partial(first_kernel, ngx, nyz, w),
        out_shape=[
            jax.ShapeDtypeStruct((ngx, r, ff), BF),
            jax.ShapeDtypeStruct((nyz, seqs, width), BF),
        ],
        in_specs=[VM, VM, ANY, ANY, ANY],
        out_specs=[VM, VM],
        scratch_shapes=[
            pltpu.VMEM((slots, depth, w), BF), DMA((slots,)),
            pltpu.VMEM((ngx, r, width), BF), pltpu.VMEM((h, r, width), BF),
            pltpu.VMEM((g, r, width), BF), pltpu.VMEM((g, r, width), BF),
            DMA((h,)), DMA((h,)), DMA((g,)), DMA((g,)),
            pltpu.VMEM((nyz, seqs, width), BF), DMA((nyz - 1,)), DMA((nyz - 1,)),
            pltpu.VMEM((nc, ngx, r, 2 * w), BF), pltpu.VMEM((nc, h, r, 2 * w), BF),
            pltpu.VMEM((nc, g, r, 2 * w), BF), pltpu.VMEM((nc, g, r, 2 * w), BF),
            DMA((nc, h)), DMA((nc, h)), DMA((nc, g)), DMA((nc, g)),
            DMA((nc, g)), DMA((nc, g)), DMA((nc, h)), DMA((nc, h)),
        ],
        compiler_params=params(1),
        name="project",
    )(x, kv, qw, gw, uw)


def second_kernel(ngx, nyz, wd, wo, hid_ref, att_ref, dw, ow, out_ref,
                  dbuf, dsem, obuf, osem, acc, sw, ssem, rsem, heads, sa, ra, sb, rb,
                  px, p1, ps, p2, psem1, psem2, psem3, psem4):
    tx, ty = Pairs("gx", ngx), Pairs("yz", nyz)
    cols = dw.shape[1]
    nd, no = cols // wd, cols // wo
    r, qc = heads.shape[1], heads.shape[2]
    seqs = att_ref.shape[1]
    slots = dbuf.shape[0]

    def fetch(i):
        return pltpu.make_async_copy(dw.at[:, pl.ds(i * wd, wd)], dbuf.at[i % slots], dsem.at[i % slots])

    def fetch_out(i):
        return pltpu.make_async_copy(ow.at[:, pl.ds(i * wo, wo)], obuf.at[i], osem.at[i])

    for i in range(min(slots, nd)):
        fetch(i).start()
    swap = Swap("yz", nyz, att_ref, sw, ssem, rsem)
    greet(tx.all() + swap.peers)
    swap.start()
    gat = Gather(tx, lambda i: heads.at[i], sa, ra, sb, rb)

    def join():
        swap.end()
        heads[tx.me] = jnp.concatenate([sw[i].astype(F32) for i in range(nyz)], axis=0).astype(BF)
        gat.start()

    jobs = {2: join, 5: gat.pass_on}
    hid = hid_ref[...]
    for i in range(nd):
        fetch(i).wait()
        acc[:, i * wd:(i + 1) * wd] = jnp.dot(hid, dbuf[i % slots], preferred_element_type=F32)
        if i + slots < nd:
            fetch(i + slots).start()
        elif i + slots - nd < no:
            fetch_out(i + slots - nd).start()
        if i in jobs:
            jobs[i]()
    gat.end()
    att = heads[...].reshape(ngx * r, qc)
    reds = [
        Reduce(ty, px.at[c], p1.at[c], ps.at[c], p2.at[c], psem1.at[c], psem2.at[c], psem3.at[c], psem4.at[c])
        for c in range(no)
    ]
    rows = out_ref.shape[0]
    for c in range(no):
        fetch_out(c).wait()
        y = acc[:, c * wo:(c + 1) * wo] + jnp.dot(att, obuf[c], preferred_element_type=F32)
        px[c] = y.astype(BF).reshape(nyz, rows, wo)
        reds[c].start()
        if c > 0:
            reds[c - 1].pass_on()
    reds[no - 1].pass_on()
    for c in range(no):
        out_ref[:, c * wo:(c + 1) * wo] = reds[c].total()
    for c in range(no):
        reds[c].end()


def second(hid, att, dw, ow, ngx, nyz):
    batch, ff = hid.shape
    _, seqs, qc = att.shape
    cols = dw.shape[1]
    wd, wo = 256, 768
    no = cols // wo
    rx, r, hx, hy = batch // ngx, batch // nyz, ngx // 2, nyz // 2
    gx, gy = max(hx - 1, 1), max(hy - 1, 1)
    slots = 4
    ANY = pl.BlockSpec(memory_space=pl.ANY)
    return pl.pallas_call(
        functools.partial(second_kernel, ngx, nyz, wd, wo),
        out_shape=jax.ShapeDtypeStruct((r, cols), F32),
        in_specs=[VM, VM, ANY, ANY],
        out_specs=VM,
        scratch_shapes=[
            pltpu.VMEM((slots, ff, wd), BF), DMA((slots,)),
            pltpu.VMEM((no, qc, wo), BF), DMA((no,)),
            pltpu.VMEM((batch, cols), F32),
            pltpu.VMEM((nyz, seqs, qc), BF), DMA((nyz - 1,)), DMA((nyz - 1,)),
            pltpu.VMEM((ngx, rx, qc), BF), DMA((gx,)), DMA((gx,)), DMA((hx,)), DMA((hx,)),
            pltpu.VMEM((no, nyz, r, wo), BF), pltpu.VMEM((no, hy, r, wo), BF),
            pltpu.VMEM((no, gy, r, wo), BF), pltpu.VMEM((no, gy, r, wo), BF),
            DMA((no, hy)), DMA((no, hy)), DMA((no, gy)), DMA((no, gy)),
        ],
        compiler_params=params(2),
        name="combine",
    )(hid, att, dw, ow)


def attend_local(query, new_kv, cache, lengths):
    seqs = query.shape[0]
    head_dim = cache.shape[2] // 2
    heads = query.shape[1] // head_dim
    query_vectors = query.reshape(seqs, heads, head_dim)
    key_rows = cache[:, :, :head_dim]
    value_rows = cache[:, :, head_dim:]
    new_key = new_kv[:, :head_dim]
    new_value = new_kv[:, head_dim:]
    score_scale = 1.0 / math.sqrt(head_dim)
    attention_logits = (
        jnp.einsum("tgb,twb->tgw", query_vectors, key_rows, preferred_element_type=jnp.float32)
        * score_scale
    )
    own = (
        jnp.einsum("shd,sd->sh", query_vectors, new_key, preferred_element_type=jnp.float32)
        * score_scale
    )
    positions = lax.broadcasted_iota(jnp.int32, (1, 1, cache.shape[1]), 2)
    valid = positions < lengths[:, None, None]
    top = jnp.maximum(jnp.max(jnp.where(valid, attention_logits, own[:, :, None]), axis=2), own)
    weights = jnp.where(valid, jnp.exp(attention_logits - top[:, :, None]), jnp.float32(0.0))
    own_weight = jnp.exp(own - top)
    denom = jnp.sum(weights, axis=2) + own_weight
    attention_probabilities = (weights / denom[:, :, None]).astype(jnp.bfloat16)
    own_prob = (own_weight / denom).astype(jnp.bfloat16)
    value_mixture = jnp.einsum(
        "aqc,acn->aqn", attention_probabilities, value_rows, preferred_element_type=jnp.float32
    )
    value_mixture = (
        value_mixture
        + own_prob.astype(jnp.float32)[:, :, None] * new_value.astype(jnp.float32)[:, None, :]
    )
    return value_mixture.astype(jnp.bfloat16).reshape(seqs, heads * head_dim)


def body(ngx, nyz, stream, ln_gain, q_weight, kv_weight, out_weight, gate_weight, up_weight,
         down_weight, cache, lengths):
    normed = norm_gather(stream, ln_gain, ngx, nyz)
    batch = normed.shape[0]
    qc, kc = q_weight.shape[1], kv_weight.shape[1]
    pad = -(qc + kc) % 128
    seqs = batch // ngx // nyz

    kv_part = jnp.dot(normed, kv_weight, preferred_element_type=F32).astype(BF)
    kv_part = jnp.pad(kv_part, ((0, 0), (0, pad)))
    hidden, qkv_own = first(normed, kv_part, q_weight, gate_weight, up_weight, ngx, nyz)
    qkv_own = jnp.swapaxes(qkv_own, 0, 1)
    query_own = qkv_own[:, :, :qc].reshape(seqs, nyz * qc)
    kv_own = qkv_own[:, :, qc:qc + kc].reshape(seqs, nyz * kc)
    attended = attend_local(query_own, kv_own, cache, lengths)
    blocks = jnp.swapaxes(attended.reshape(seqs, nyz, qc), 0, 1)
    update = second(hidden.reshape(batch, -1), blocks, down_weight, out_weight, ngx, nyz)
    return update.astype(BF)


def solution(mesh):
    ngx, nyz = mesh.shape["gx"], mesh.shape["yz"]
    return jax.shard_map(
        functools.partial(body, ngx, nyz),
        mesh=mesh,
        in_specs=(
            P("yz", "gx"),
            P("gx"),
            P("gx", "yz"),
            P("gx", "yz"),
            P("yz", "gx"),
            P("gx", "yz"),
            P("gx", "yz"),
            P("yz", "gx"),
            P(("gx", "yz"), None, None),
            P(("gx", "yz")),
        ),
        out_specs=P("yz", "gx"),
        check_vma=False,
    )
```

```python
import functools
import math

import jax
import jax.numpy as jnp
from jax import lax
from jax.experimental import pallas as pl
from jax.experimental.pallas import tpu as pltpu
from jax.sharding import PartitionSpec as P

D = 9216
BF = jnp.bfloat16
F32 = jnp.float32
MESH = pl.DeviceIdType.MESH


def greet(peers):
    barrier = pltpu.get_barrier_semaphore()
    for peer in peers:
        pl.semaphore_signal(barrier, inc=1, device_id=peer, device_id_type=MESH)
    pl.semaphore_wait(barrier, len(peers))


def remote(src, dst, send, recv, peer):
    return pltpu.make_async_remote_copy(
        src_ref=src, dst_ref=dst, send_sem=send, recv_sem=recv,
        device_id=peer, device_id_type=MESH,
    )


class Pairs:
    def __init__(self, axis, n):
        self.axis, self.n, self.half = axis, n, n // 2
        self.me = lax.axis_index(axis)
        self.place = lax.rem(self.me, 2)
        self.row = lax.div(self.me, 2)
        self.partner = {axis: self.me + 1 - 2 * self.place}

    def ahead(self, j):
        return lax.rem(self.row + 1 + j, self.half)

    def behind(self, j):
        return lax.rem(self.row + 2 * self.half - 1 - j, self.half)

    def peer(self, j):
        return {self.axis: 2 * self.ahead(j) + self.place}

    def all(self):
        return [self.partner] + [self.peer(j) for j in range(self.half - 1)]


def gather_start(t, src, out, sa, ra, sb, rb):
    copies = []
    for j in range(t.half - 1):
        c = remote(src, out.at[t.me], sa.at[j], ra.at[j], t.peer(j))
        c.start()
        copies.append(c)
    c = remote(src, out.at[t.me], sb.at[0], rb.at[0], t.partner)
    c.start()
    return copies, [c]


def gather_finish(t, out, sa, ra, sb, rb, started):
    first, second = started
    for j in range(t.half - 1):
        got = 2 * t.behind(j) + t.place
        remote(out.at[got], out.at[got], sa.at[j], ra.at[j], t.peer(j)).wait_recv()
        c = remote(out.at[got], out.at[got], sb.at[1 + j], rb.at[1 + j], t.partner)
        c.start()
        second.append(c)
    for c in first:
        c.wait_send()
    for c in second:
        c.wait()


def normalize(t, others, x_ref, gain_ref, out_ref, stat, got, ss, sr, sa, ra, sb, rb):
    rows = x_ref.shape[0]
    x = x_ref[...].astype(F32)
    stat[0] = jnp.broadcast_to(jnp.sum(x, axis=1, keepdims=True), (rows, 128))
    stat[1] = jnp.broadcast_to(jnp.sum(x * x, axis=1, keepdims=True), (rows, 128))
    copies = []
    for j in range(len(others)):
        c = remote(stat, got.at[j], ss.at[j], sr.at[j], others[j])
        c.start()
        copies.append(c)
    for c in copies:
        c.wait()
    total = stat[0]
    squares = stat[1]
    for j in range(len(others)):
        total = total + got[j, 0]
        squares = squares + got[j, 1]
    mean = total[:, :1] / D
    var = squares[:, :1] / D - mean * mean
    normed = (x - mean) * lax.rsqrt(var + 1e-05) * gain_ref[...].astype(F32)
    out_ref[t.me] = normed.astype(BF)
    started = gather_start(t, out_ref.at[t.me], out_ref, sa, ra, sb, rb)
    gather_finish(t, out_ref, sa, ra, sb, rb, started)


DMA = pltpu.SemaphoreType.DMA
VM = pl.BlockSpec(memory_space=pltpu.VMEM)


def params(cid):
    return pltpu.CompilerParams(
        collective_id=cid, has_side_effects=True, vmem_limit_bytes=52 * 1024 * 1024
    )


def reduce_start(t, x_ref, recv1, s1, r1):
    copies = []
    for j in range(t.half):
        k = t.ahead(j)
        c = remote(x_ref.at[2 * k + 1 - t.place], recv1.at[j], s1.at[j], r1.at[j], t.partner)
        c.start()
        copies.append(c)
    return copies


class Reduce:
    def __init__(self, t, x, recv1, stage, recv2, s1, r1, s2, r2):
        self.t, self.x, self.recv1, self.stage, self.recv2 = t, x, recv1, stage, recv2
        self.s1, self.r1, self.s2, self.r2 = s1, r1, s2, r2

    def start(self):
        self.first = reduce_start(self.t, self.x, self.recv1, self.s1, self.r1)

    def pass_on(self):
        t = self.t
        self.second = []
        for j in range(t.half - 1):
            k = t.ahead(j)
            self.first[j].wait_recv()
            self.stage[j] = (
                self.x[2 * k + t.place].astype(F32) + self.recv1[j].astype(F32)
            ).astype(BF)
            c = remote(self.stage.at[j], self.recv2.at[j], self.s2.at[j], self.r2.at[j], t.peer(j))
            c.start()
            self.second.append(c)

    def total(self):
        t = self.t
        self.first[t.half - 1].wait_recv()
        total = self.x[t.me].astype(F32) + self.recv1[t.half - 1].astype(F32)
        for j in range(t.half - 1):
            self.second[j].wait_recv()
            total = total + self.recv2[j].astype(F32)
        return total

    def end(self):
        for c in self.first + self.second:
            c.wait_send()


class Gather:
    def __init__(self, t, view, sa, ra, sb, rb):
        self.t, self.view = t, view
        self.sa, self.ra, self.sb, self.rb = sa, ra, sb, rb

    def start(self):
        t, own = self.t, self.view(self.t.me)
        self.first = []
        for j in range(t.half - 1):
            c = remote(own, own, self.sa.at[j], self.ra.at[j], t.peer(j))
            c.start()
            self.first.append(c)
        c = remote(own, own, self.sb.at[0], self.rb.at[0], t.partner)
        c.start()
        self.second = [c]

    def pass_on(self):
        t = self.t
        for j in range(t.half - 1):
            got = self.view(2 * t.behind(j) + t.place)
            remote(got, got, self.sa.at[j], self.ra.at[j], t.peer(j)).wait_recv()
            c = remote(got, got, self.sb.at[1 + j], self.rb.at[1 + j], t.partner)
            c.start()
            self.second.append(c)

    def end(self):
        for c in self.first:
            c.wait_send()
        for c in self.second:
            c.wait()


class Swap:
    def __init__(self, axis, n, src, dst, ss, rs):
        self.me = lax.axis_index(axis)
        self.n, self.src, self.dst, self.ss, self.rs = n, src, dst, ss, rs
        self.ids = [lax.rem(self.me + 1 + j, n) for j in range(n - 1)]
        self.peers = [{axis: i} for i in self.ids]

    def start(self):
        self.copies = []
        for j in range(self.n - 1):
            c = remote(
                self.src.at[self.ids[j]], self.dst.at[self.me], self.ss.at[j], self.rs.at[j],
                self.peers[j],
            )
            c.start()
            self.copies.append(c)
        self.dst[self.me] = self.src[self.me]

    def end(self):
        for c in self.copies:
            c.wait()


def first_kernel(ngx, nyz, w, s_ref, gain_ref, kvw, qw, gw, uw, hid, own,
                 xg, stat, got, nss, nsr, nsa, nra, nsb, nrb,
                 wbuf, wsem, qx, q1, qs, q2, qsem1, qsem2, qsem3, qsem4, sw, ssem, rsem,
                 px, p1, ps, p2, psem1, psem2, psem3, psem4, sa, ra, sb, rb):
    t = Pairs("gx", ngx)
    qc, ff = qw.shape[1], gw.shape[1]
    nq, nc = qc // w, ff // w
    r = hid.shape[1]
    slots = wbuf.shape[0]
    tiles = [(qw, i) for i in range(nq)]
    for c in range(nc):
        tiles += [(gw, c), (uw, c)]

    def fetch(i):
        ref, c = tiles[i]
        return pltpu.make_async_copy(ref.at[:, pl.ds(c * w, w)], wbuf.at[i % slots], wsem.at[i % slots])

    for i in range(min(slots, len(tiles))):
        fetch(i).start()
    swap = Swap("yz", nyz, sw, own, ssem, rsem)
    others = [{"gx": lax.rem(t.me + 1 + j, ngx)} for j in range(ngx - 1)]
    greet(others + swap.peers)
    normalize(Pairs("yz", nyz), others, s_ref, gain_ref, xg, stat, got, nss, nsr, nsa, nra, nsb, nrb)

    jobs = {}

    def at(step, rank, f):
        jobs.setdefault(step, []).append((rank, f))

    qred = Reduce(t, qx, q1, qs, q2, qsem1, qsem2, qsem3, qsem4)
    reds = [
        Reduce(t, px.at[c], p1.at[c], ps.at[c], p2.at[c], psem1.at[c], psem2.at[c], psem3.at[c], psem4.at[c])
        for c in range(nc)
    ]
    gats = [
        Gather(t, lambda i, c=c: hid.at[i, :, pl.ds(c * w, w)], sa.at[c], ra.at[c], sb.at[c], rb.at[c])
        for c in range(nc)
    ]

    def q_total():
        total = qred.total()
        seqs = sw.shape[1]
        for i in range(nyz):
            sw[i] = total[i * seqs:(i + 1) * seqs].astype(BF)
        swap.start()

    def h_total(c):
        both = reds[c].total()
        hid[t.me, :, c * w:(c + 1) * w] = (jax.nn.silu(both[:, :w]) * both[:, w:]).astype(BF)
        gats[c].start()

    at(nq - 1, 0, qred.start)
    at(nq, 1, qred.pass_on)
    at(nq + 3, 2, q_total)
    for c in range(nc):
        s = nq + 2 * c + 1
        at(s, 0, reds[c].start)
        at(s + 1, 1, reds[c].pass_on)
        at(s + 4, 2, lambda c=c: h_total(c))
        at(s + 7, 3, gats[c].pass_on)

    x = xg[...].reshape(ngx * r, xg.shape[2])
    for i in range(max(jobs) + 1):
        if i < len(tiles):
            fetch(i).wait()
            y = jnp.dot(x, wbuf[i % slots], preferred_element_type=F32).astype(BF).reshape(ngx, r, w)
            if i < nq:
                qx[:, :, i * w:(i + 1) * w] = y
            else:
                side = (i - nq) % 2
                px[(i - nq) // 2, :, :, side * w:(side + 1) * w] = y
            if i + slots < len(tiles):
                fetch(i + slots).start()
            if i == nq - 1:
                kv = jnp.dot(x, kvw[...], preferred_element_type=F32).astype(BF)
                qx[:, :, qc:] = kv.reshape(ngx, r, kv.shape[1])
        for _, f in sorted(jobs.get(i, []), key=lambda job: job[0]):
            f()
    for c in range(nc):
        reds[c].end()
        gats[c].end()
    qred.end()
    swap.end()


def first(x, gain, kv, qw, gw, uw, ngx, nyz):
    rows, depth = x.shape
    batch, hy = rows * nyz, nyz // 2
    gy = max(hy - 1, 1)
    qc, ff = qw.shape[1], gw.shape[1]
    w = 768 if qc % 768 == 0 and ff % 768 == 0 else 384
    nc = ff // w
    r, h = batch // ngx, ngx // 2
    g = max(h - 1, 1)
    seqs = r // nyz
    width = qc + kv.shape[1]
    slots = 9
    ANY = pl.BlockSpec(memory_space=pl.ANY)
    return pl.pallas_call(
        functools.partial(first_kernel, ngx, nyz, w),
        out_shape=[
            jax.ShapeDtypeStruct((ngx, r, ff), BF),
            jax.ShapeDtypeStruct((nyz, seqs, width), BF),
        ],
        in_specs=[VM, VM, VM, ANY, ANY, ANY],
        out_specs=[VM, VM],
        scratch_shapes=[
            pltpu.VMEM((nyz, rows, depth), BF), pltpu.VMEM((2, rows, 128), F32),
            pltpu.VMEM((ngx - 1, 2, rows, 128), F32), DMA((ngx - 1,)), DMA((ngx - 1,)),
            DMA((gy,)), DMA((gy,)), DMA((hy,)), DMA((hy,)),
            pltpu.VMEM((slots, depth, w), BF), DMA((slots,)),
            pltpu.VMEM((ngx, r, width), BF), pltpu.VMEM((h, r, width), BF),
            pltpu.VMEM((g, r, width), BF), pltpu.VMEM((g, r, width), BF),
            DMA((h,)), DMA((h,)), DMA((g,)), DMA((g,)),
            pltpu.VMEM((nyz, seqs, width), BF), DMA((nyz - 1,)), DMA((nyz - 1,)),
            pltpu.VMEM((nc, ngx, r, 2 * w), BF), pltpu.VMEM((nc, h, r, 2 * w), BF),
            pltpu.VMEM((nc, g, r, 2 * w), BF), pltpu.VMEM((nc, g, r, 2 * w), BF),
            DMA((nc, h)), DMA((nc, h)), DMA((nc, g)), DMA((nc, g)),
            DMA((nc, g)), DMA((nc, g)), DMA((nc, h)), DMA((nc, h)),
        ],
        compiler_params=params(1),
        name="project",
    )(x, gain.reshape(1, depth), kv, qw, gw, uw)


def second_kernel(ngx, nyz, wd, wo, hid_ref, att_ref, dw, ow, out_ref,
                  dbuf, dsem, obuf, osem, acc, sw, ssem, rsem, heads, sa, ra, sb, rb,
                  px, p1, ps, p2, psem1, psem2, psem3, psem4):
    tx, ty = Pairs("gx", ngx), Pairs("yz", nyz)
    cols = dw.shape[1]
    nd, no = cols // wd, cols // wo
    r, qc = heads.shape[1], heads.shape[2]
    seqs = att_ref.shape[1]
    slots = dbuf.shape[0]

    def fetch(i):
        return pltpu.make_async_copy(dw.at[:, pl.ds(i * wd, wd)], dbuf.at[i % slots], dsem.at[i % slots])

    def fetch_out(i):
        return pltpu.make_async_copy(ow.at[:, pl.ds(i * wo, wo)], obuf.at[i], osem.at[i])

    for i in range(min(slots, nd)):
        fetch(i).start()
    swap = Swap("yz", nyz, att_ref, sw, ssem, rsem)
    greet(tx.all() + swap.peers)
    swap.start()
    gat = Gather(tx, lambda i: heads.at[i], sa, ra, sb, rb)

    def join():
        swap.end()
        heads[tx.me] = jnp.concatenate([sw[i].astype(F32) for i in range(nyz)], axis=0).astype(BF)
        gat.start()

    jobs = {3: join, 7: gat.pass_on}
    hid = hid_ref[...]
    for i in range(nd):
        fetch(i).wait()
        acc[:, i * wd:(i + 1) * wd] = jnp.dot(hid, dbuf[i % slots], preferred_element_type=F32)
        if i + slots < nd:
            fetch(i + slots).start()
        elif i + slots - nd < no:
            fetch_out(i + slots - nd).start()
        if i in jobs:
            jobs[i]()
    gat.end()
    att = heads[...].reshape(ngx * r, qc)
    reds = [
        Reduce(ty, px.at[c], p1.at[c], ps.at[c], p2.at[c], psem1.at[c], psem2.at[c], psem3.at[c], psem4.at[c])
        for c in range(no)
    ]
    rows = out_ref.shape[0]
    for c in range(no):
        fetch_out(c).wait()
        y = acc[:, c * wo:(c + 1) * wo] + jnp.dot(att, obuf[c], preferred_element_type=F32)
        px[c] = y.astype(BF).reshape(nyz, rows, wo)
        reds[c].start()
        if c > 0:
            reds[c - 1].pass_on()
    reds[no - 1].pass_on()
    for c in range(no):
        out_ref[:, c * wo:(c + 1) * wo] = reds[c].total()
    for c in range(no):
        reds[c].end()


def second(hid, att, dw, ow, ngx, nyz):
    batch, ff = hid.shape
    _, seqs, qc = att.shape
    cols = dw.shape[1]
    wd, wo = 256, 768
    no = cols // wo
    rx, r, hx, hy = batch // ngx, batch // nyz, ngx // 2, nyz // 2
    gx, gy = max(hx - 1, 1), max(hy - 1, 1)
    slots = 9
    ANY = pl.BlockSpec(memory_space=pl.ANY)
    return pl.pallas_call(
        functools.partial(second_kernel, ngx, nyz, wd, wo),
        out_shape=jax.ShapeDtypeStruct((r, cols), F32),
        in_specs=[VM, VM, ANY, ANY],
        out_specs=VM,
        scratch_shapes=[
            pltpu.VMEM((slots, ff, wd), BF), DMA((slots,)),
            pltpu.VMEM((no, qc, wo), BF), DMA((no,)),
            pltpu.VMEM((batch, cols), F32),
            pltpu.VMEM((nyz, seqs, qc), BF), DMA((nyz - 1,)), DMA((nyz - 1,)),
            pltpu.VMEM((ngx, rx, qc), BF), DMA((gx,)), DMA((gx,)), DMA((hx,)), DMA((hx,)),
            pltpu.VMEM((no, nyz, r, wo), BF), pltpu.VMEM((no, hy, r, wo), BF),
            pltpu.VMEM((no, gy, r, wo), BF), pltpu.VMEM((no, gy, r, wo), BF),
            DMA((no, hy)), DMA((no, hy)), DMA((no, gy)), DMA((no, gy)),
        ],
        compiler_params=params(2),
        name="combine",
    )(hid, att, dw, ow)


def attend_local(query, new_kv, cache, lengths):
    seqs = query.shape[0]
    head_dim = cache.shape[2] // 2
    heads = query.shape[1] // head_dim
    query_vectors = query.reshape(seqs, heads, head_dim)
    key_rows = cache[:, :, :head_dim]
    value_rows = cache[:, :, head_dim:]
    new_key = new_kv[:, :head_dim]
    new_value = new_kv[:, head_dim:]
    score_scale = 1.0 / math.sqrt(head_dim)
    attention_logits = (
        jnp.einsum("tgb,twb->tgw", query_vectors, key_rows, preferred_element_type=jnp.float32)
        * score_scale
    )
    own = (
        jnp.einsum("shd,sd->sh", query_vectors, new_key, preferred_element_type=jnp.float32)
        * score_scale
    )
    positions = lax.broadcasted_iota(jnp.int32, (1, 1, cache.shape[1]), 2)
    valid = positions < lengths[:, None, None]
    top = jnp.maximum(jnp.max(jnp.where(valid, attention_logits, own[:, :, None]), axis=2), own)
    weights = jnp.where(valid, jnp.exp(attention_logits - top[:, :, None]), jnp.float32(0.0))
    own_weight = jnp.exp(own - top)
    denom = jnp.sum(weights, axis=2) + own_weight
    attention_probabilities = (weights / denom[:, :, None]).astype(jnp.bfloat16)
    own_prob = (own_weight / denom).astype(jnp.bfloat16)
    value_mixture = jnp.einsum(
        "aqc,acn->aqn", attention_probabilities, value_rows, preferred_element_type=jnp.float32
    )
    value_mixture = (
        value_mixture
        + own_prob.astype(jnp.float32)[:, :, None] * new_value.astype(jnp.float32)[:, None, :]
    )
    return value_mixture.astype(jnp.bfloat16).reshape(seqs, heads * head_dim)


def body(ngx, nyz, stream, ln_gain, q_weight, kv_weight, out_weight, gate_weight, up_weight,
         down_weight, cache, lengths):
    batch = stream.shape[0] * nyz
    qc, kc = q_weight.shape[1], kv_weight.shape[1]
    pad = -(qc + kc) % 128
    seqs = batch // ngx // nyz
    kv_padded = jnp.pad(kv_weight, ((0, 0), (0, pad)))
    hidden, qkv_own = first(
        stream, ln_gain, kv_padded, q_weight, gate_weight, up_weight, ngx, nyz
    )
    qkv_own = jnp.swapaxes(qkv_own, 0, 1)
    query_own = qkv_own[:, :, :qc].reshape(seqs, nyz * qc)
    kv_own = qkv_own[:, :, qc:qc + kc].reshape(seqs, nyz * kc)
    attended = attend_local(query_own, kv_own, cache, lengths)
    blocks = jnp.swapaxes(attended.reshape(seqs, nyz, qc), 0, 1)
    update = second(hidden.reshape(batch, -1), blocks, down_weight, out_weight, ngx, nyz)
    return update.astype(BF)


def solution(mesh):
    ngx, nyz = mesh.shape["gx"], mesh.shape["yz"]
    return jax.shard_map(
        functools.partial(body, ngx, nyz),
        mesh=mesh,
        in_specs=(
            P("yz", "gx"),
            P("gx"),
            P("gx", "yz"),
            P("gx", "yz"),
            P("yz", "gx"),
            P("gx", "yz"),
            P("gx", "yz"),
            P("yz", "gx"),
            P(("gx", "yz"), None, None),
            P(("gx", "yz")),
        ),
        out_specs=P("yz", "gx"),
        check_vma=False,
    )
```
